128 devices in a mesh: section: 2 (over x_hi), rows: 16 (over y, x_lo, core), cols: 4 (over z).
Axes of the slice: x: 4 (x_hi: 2, x_lo: 2; x = x_hi * 2 + x_lo), y: 4, z: 4, core: 2. Of those that a mesh axis runs over, the one named last changes fastest.
Arguments:
- features: bfloat16 [2, 384, 96, 728], P(None, ('rows', 'cols')), may hold values from -6 to 6
- upstream: bfloat16 [2, 384, 96, 256], P(None, 'rows', 'cols'), may hold values from -0.0234375 to 0.0234375
- depth_mid: float32 [9, 728], replicated, may hold values from -2 to 2
- point_mid: bfloat16 [728, 728], replicated, may hold values from -0.21875 to 0.21875
- projection: bfloat16 [728, 2048], replicated, may hold values from -0.21875 to 0.21875
- depth_first: float32 [9, 2048], replicated, may hold values from -2 to 2
- point_first: bfloat16 [2048, 256], replicated, may hold values from -0.125 to 0.125
- depth_later: float32 [2, 9, 256], replicated, may hold values from -2 to 2
- point_later: bfloat16 [2, 256, 256], replicated, may hold values from -0.375 to 0.375
- joining: bfloat16 [768, 256], replicated, may hold values from -0.21875 to 0.21875
- rate_first: int32 [2], replicated, may hold values from 1 to 6, as said below
- rates_later: int32 [2, 2], replicated, may hold values from 1 to 21, as said below
Outputs:
- grad_mid: float32 [728, 728], replicated
- grad_later: float32 [2, 256, 256], replicated
The draws below stay inside these ranges and needn't reach their ends.
Inputs may be any that keep to these rules, and one draw needn't show every extreme that they name: `rate_first`: at least one of the two rates equals 6. `rates_later`: at least one of the rates equals 21.
All inputs are finite; a program needn't handle non-finite values.
Results may differ from the reference program's by a relative error of at most 0.015.
Values may be sent and summed in bfloat16 or wider, within the bound.
No kernel may reach another device: no remote copies, remote signals or barrier semaphores. Data moves between devices by JAX's collectives and lax.ppermute only.
A program may use at most 128 MiB of HBM per device.

```python
import jax
import jax.numpy as jnp
from jax import lax

C = 728
CH = 2048
B = 256
LATER = 2
R0 = 6
RMAX = 21
MB = 2
H = 384
W = 96


def draw_rate_first(key, part):
    values = jax.random.randint(key, (2,), 1, R0 + 1)
    chosen = jax.random.randint(jax.random.fold_in(key, 11), (), 0, 2)
    return jnp.where(jnp.arange(2) == chosen, R0, values).astype(jnp.int32)


def draw_rates_later(key, part):
    values = jax.random.randint(key, (LATER, 2), 1, RMAX + 1)
    chosen = jax.random.randint(jax.random.fold_in(key, 13), (), 0, LATER * 2)
    places = jnp.arange(LATER * 2).reshape(LATER, 2)
    return jnp.where(places == chosen, RMAX, values).astype(jnp.int32)


def levels(rng, dims, cuts, smallest, high):
    def one(dim, blocks):
        steps = jax.random.uniform(jax.random.fold_in(jax.random.fold_in(rng, 6), dim), (blocks,), jnp.float32, smallest / len(cuts), high / len(cuts))
        return jnp.repeat(jnp.exp(steps), dims[dim] // blocks).reshape((-1,) + (1,) * (len(dims) - dim - 1))

    factor_of = one(*cuts[0])
    for cut in cuts[1:]:
        factor_of = factor_of * one(*cut)
    return factor_of


def centred(key, extent, spread, bound, split=(), held_as=jnp.bfloat16):
    entries = spread * jax.random.normal(key, extent, jnp.float32)
    if split:
        entries = entries * levels(key, extent, split, -0.22, 0.18)
    return jnp.clip(entries, -bound, bound).astype(held_as)


def setup_inputs(seed: int = 0) -> dict:
    key_list = jax.random.split(jax.random.key(seed), 13)
    return {
        "features": centred(key_list[0], (MB, H, W, C), 1.0, 6.0, ((1, 64),)),
        "upstream": centred(key_list[1], (MB, H, W, B), ((MB * H * W) ** -0.5), 0.0234375, ((1, 16), (2, 4))),
        "depth_mid": centred(key_list[2], (9, C), 9 ** -0.5, 2.0, (), jnp.float32),
        "point_mid": centred(key_list[3], (C, C), C ** -0.5, 0.21875),
        "projection": centred(key_list[4], (C, CH), C ** -0.5, 0.21875),
        "depth_first": centred(key_list[5], (9, CH), 9 ** -0.5, 2.0, (), jnp.float32),
        "point_first": centred(key_list[6], (CH, B), CH ** -0.5, 0.125),
        "depth_later": centred(key_list[7], (LATER, 9, B), 9 ** -0.5, 2.0, (), jnp.float32),
        "point_later": centred(key_list[8], (LATER, B, B), B ** -0.5, 0.375),
        "joining": centred(key_list[9], ((LATER + 1) * B, B), ((LATER + 1) * B) ** -0.5, 0.21875),
        "rate_first": draw_rate_first(jax.random.fold_in(key_list[12], 71), 0),
        "rates_later": draw_rates_later(jax.random.fold_in(key_list[12], 71), 0),
    }


def silu_slope(argument):
    sigmoid_value = jax.nn.sigmoid(argument)
    return sigmoid_value * (1.0 + argument * (1.0 - sigmoid_value))


def dilated(field, weights, rates_pair, margin, direction):
    padded = jnp.pad(field, ((margin, margin), (margin, margin), (0, 0)))
    height, breadth, depth = field.shape
    summed = jnp.zeros(field.shape, jnp.float32)
    for row_step in (-1, 0, 1):
        for col_step in (-1, 0, 1):
            row_start = (margin + direction * row_step * rates_pair[0]).astype(jnp.int32)
            col_start = (margin + direction * col_step * rates_pair[1]).astype(jnp.int32)
            window = lax.dynamic_slice(padded, (row_start, col_start, jnp.zeros((), jnp.int32)), (height, breadth, depth))
            summed = summed + window.astype(jnp.float32) * weights[3 * (row_step + 1) + col_step + 1]
    return summed


def matmul(left, right):
    flat = left.reshape(-1, left.shape[2])
    result = jnp.dot(flat, right, preferred_element_type=jnp.float32)
    return result.reshape(left.shape[0], left.shape[1], right.shape[1])


def gram(left, right):
    return jnp.dot(left.reshape(-1, left.shape[2]).T, right.reshape(-1, right.shape[2]), preferred_element_type=jnp.float32)


def reference(features, upstream, depth_mid, point_mid, projection, depth_first, point_first, depth_later, point_later, joining, rate_first, rates_later):
    unit_rates = jnp.ones((2,), jnp.int32)
    channels = point_later.shape[1]

    def micro_batch(operands):
        features_now, upstream_now = operands
        activated = jax.nn.silu(features_now.astype(jnp.float32))
        mid_conv = dilated(activated, depth_mid, unit_rates, 1, 1).astype(jnp.bfloat16)
        section_out = (features_now.astype(jnp.float32) + matmul(mid_conv, point_mid)).astype(jnp.bfloat16)
        projected = matmul(section_out, projection).astype(jnp.bfloat16)
        first_conv = dilated(projected, depth_first, rate_first, R0, 1).astype(jnp.bfloat16)
        first_pre = matmul(first_conv, point_first)
        first_out = jax.nn.silu(first_pre).astype(jnp.bfloat16)
        upstream_back = matmul(upstream_now, joining.T)
        first_back = upstream_back[:, :, :channels]
        branch_grads = []
        for branch in range(LATER):
            later_conv = dilated(first_out, depth_later[branch], rates_later[branch], RMAX, 1).astype(jnp.bfloat16)
            later_pre = matmul(later_conv, point_later[branch])
            block = upstream_back[:, :, (branch + 1) * channels:(branch + 2) * channels]
            later_gate = (block * silu_slope(later_pre)).astype(jnp.bfloat16)
            later_back = matmul(later_gate, point_later[branch].T).astype(jnp.bfloat16)
            branch_grads.append(gram(later_conv, later_gate))
            first_back = first_back + dilated(later_back, depth_later[branch], rates_later[branch], RMAX, -1)
        first_gate = (first_back * silu_slope(first_pre)).astype(jnp.bfloat16)
        conv_back = matmul(first_gate, point_first.T).astype(jnp.bfloat16)
        projected_back = dilated(conv_back, depth_first, rate_first, R0, -1).astype(jnp.bfloat16)
        section_back = matmul(projected_back, projection.T).astype(jnp.bfloat16)
        return gram(mid_conv, section_back), jnp.stack(branch_grads)

    mid_terms, later_terms = lax.map(micro_batch, (features, upstream))
    return jnp.sum(mid_terms, axis=0), jnp.sum(later_terms, axis=0)
```

```python
import jax
import jax.numpy as jnp
from jax import lax
from jax.experimental import pallas as pl
from jax.experimental.pallas import tpu as pltpu
from jax.sharding import Mesh, PartitionSpec as P

BF = jnp.bfloat16
F32 = jnp.float32
SLABS = ("y", "xl", "core", "z")
CHIPS = ("xh", "y", "xl", "z")
VM = pl.BlockSpec(memory_space=pltpu.VMEM)
SM = pl.BlockSpec(memory_space=pltpu.SMEM)
NN = (((1,), (0,)), ((), ()))
NT = (((1,), (1,)), ((), ()))
TN = (((0,), (0,)), ((), ()))


def mm(a, b, dims=NN):
    return lax.dot_general(a, b, dims, preferred_element_type=F32)


def sigmoid(v):
    return 1.0 / (1.0 + jnp.exp(-v))


def slope(v):
    s = sigmoid(v)
    return s * (1.0 + v * (1.0 - s))


def shifter(width, rate):
    j = lax.broadcasted_iota(jnp.int32, (2 * width, width), 0)
    c = lax.broadcasted_iota(jnp.int32, (2 * width, width), 1)
    want = jnp.where(j < width, j - rate, j - width + rate)
    return jnp.where(c == want, 1.0, 0.0).astype(BF)


def from_slab(value, shift):
    count = lax.axis_size(SLABS)
    pairs = [(i, i - shift) for i in range(count) if 0 <= i - shift < count]
    return lax.ppermute(value, SLABS, pairs)


def weights_kernel(proj_ref, point_ref, taps_ref, out_ref):
    scaled = (point_ref[...].astype(F32) * taps_ref[0]).astype(BF)
    out_ref[0] = mm(proj_ref[...], scaled, NT).astype(BF)


def fold_weights(projection, point_first, depth_first):
    c, ch = projection.shape
    b = point_first.shape[1]
    return pl.pallas_call(
        weights_kernel,
        grid=(9,),
        in_specs=[
            pl.BlockSpec((c, ch), lambda t: (0, 0)),
            pl.BlockSpec((b, ch), lambda t: (0, 0)),
            pl.BlockSpec((1, 1, ch), lambda t: (t, 0, 0)),
        ],
        out_specs=pl.BlockSpec((1, c, b), lambda t: (t % 3, 0, t // 3)),
        out_shape=jax.ShapeDtypeStruct((3, c, 3 * b), BF),
        cost_estimate=pl.CostEstimate(
            flops=18 * c * ch * b, bytes_accessed=8 * c * ch, transcendentals=0
        ),
        name="fold_weights",
    )(projection, point_first.T, depth_first[:, None, :])


def front_kernel(
    sc_ref, feat_ref, up_ref, dn_ref, taps_ref, point_ref, m_ref,
    mid_ref, u0_ref, us_ref, act, so, left, right,
):
    part, rate = sc_ref[0], sc_ref[1]
    rows, width, c = feat_ref.shape[1:]
    zero = jnp.zeros((rows + 2, 8, c), F32)
    act[:, 0:8, :] = zero
    act[:, width + 8 : width + 16, :] = zero

    def activate(v):
        v = v.astype(F32)
        return v * sigmoid(v)

    act[0, 8 : width + 8, :] = activate(up_ref[...])
    act[rows + 1, 8 : width + 8, :] = activate(dn_ref[...])

    def fill(i, carry):
        act[i + 1, 8 : width + 8, :] = activate(feat_ref[part, i])
        return carry

    lax.fori_loop(0, rows, fill, 0)

    def conv(i, carry):
        at = pl.multiple_of(i * width, width)
        for lo in range(0, c, 128):
            hi = min(lo + 128, c)
            total = jnp.zeros((width, hi - lo), F32)
            for a in range(3):
                for b in range(3):
                    total = total + (
                        act[i + a, 7 + b : 7 + b + width, lo:hi]
                        * taps_ref[3 * a + b : 3 * a + b + 1, lo:hi]
                    )
            mid_ref[pl.ds(at, width), lo:hi] = total.astype(BF)
        return carry

    lax.fori_loop(0, rows, conv, 0)
    mixed = mm(mid_ref[...], point_ref[...])
    so[...] = (feat_ref[part].reshape(rows * width, c).astype(F32) + mixed).astype(BF)
    move = shifter(width, rate)

    def shift(i, carry):
        at = pl.ds(pl.multiple_of(i * width, width), width)
        moved = mm(move, so[at, :]).astype(BF)
        left[at, :] = moved[:width]
        right[at, :] = moved[width:]
        return carry

    lax.fori_loop(0, rows, shift, 0)
    n = u0_ref.shape[1]
    total = mm(left[...], m_ref[0]) + mm(so[...], m_ref[1]) + mm(right[...], m_ref[2])
    us_ref[0] = total[:, :n].astype(BF)
    u0_ref[...] = total[:, n : 2 * n]
    us_ref[1] = total[:, 2 * n :].astype(BF)


def front(scalars, features, up, dn, depth_mid, point_mid, folded):
    _, rows, width, c = features.shape
    n = folded.shape[2] // 3
    cells = rows * width
    return pl.pallas_call(
        front_kernel,
        in_specs=[SM] + [VM] * 6,
        out_specs=[VM] * 3,
        out_shape=[
            jax.ShapeDtypeStruct((cells, c), BF),
            jax.ShapeDtypeStruct((cells, n), F32),
            jax.ShapeDtypeStruct((2, cells, n), BF),
        ],
        scratch_shapes=[
            pltpu.VMEM((rows + 2, width + 16, c), F32),
            pltpu.VMEM((cells, c), BF),
            pltpu.VMEM((cells, c), BF),
            pltpu.VMEM((cells, c), BF),
        ],
        name="front",
    )(scalars, features, up, dn, depth_mid, point_mid, folded)


def later_kernel(
    sc_ref, own_ref, p0_ref, m0_ref, p1_ref, m1_ref, up_ref, join_ref, taps_ref, point_ref,
    back0_ref, back1_ref, grad_ref, direct_ref, conv,
):
    rows, width, n = own_ref.shape
    windows = ((m0_ref, own_ref, p0_ref), (m1_ref, own_ref, p1_ref))
    for l in range(2):
        move = shifter(width, sc_ref[l])

        def one(i, carry, l=l, move=move):
            total = jnp.zeros((width, n), F32)
            for a in range(3):
                row = windows[l][a][i]
                moved = mm(move, row)
                total = total + moved[:width] * taps_ref[l, 3 * a : 3 * a + 1, :]
                total = total + row.astype(F32) * taps_ref[l, 3 * a + 1 : 3 * a + 2, :]
                total = total + moved[width:] * taps_ref[l, 3 * a + 2 : 3 * a + 3, :]
            conv[pl.ds(pl.multiple_of(i * width, width), width), :] = total.astype(BF)
            return carry

        lax.fori_loop(0, rows, one, 0)
        pre = mm(conv[...], point_ref[l])
        block = mm(up_ref[...], join_ref[(l + 1) * n : (l + 2) * n, :], NT)
        gate = (block * slope(pre)).astype(BF)
        back = mm(gate, point_ref[l], NT).astype(BF)
        (back0_ref, back1_ref)[l][...] = back.reshape(rows, width, n)
        grad_ref[l] = mm(conv[...], gate, TN)
    direct_ref[...] = mm(up_ref[...], join_ref[:n, :], NT)


def later(rates, own, plus0, minus0, plus1, minus1, upstream, joining, depth, point):
    rows, width, n = own.shape
    cells = rows * width
    return pl.pallas_call(
        later_kernel,
        in_specs=[SM] + [VM] * 9,
        out_specs=[VM] * 4,
        out_shape=[
            jax.ShapeDtypeStruct((rows, width, n), BF),
            jax.ShapeDtypeStruct((rows, width, n), BF),
            jax.ShapeDtypeStruct((2, n, n), F32),
            jax.ShapeDtypeStruct((cells, n), F32),
        ],
        scratch_shapes=[pltpu.VMEM((cells, n), BF)],
        name="later",
    )(rates, own, plus0, minus0, plus1, minus1, upstream, joining, depth, point)


def gate_kernel(
    sc_ref, b0_ref, p0_ref, m0_ref, b1_ref, p1_ref, m1_ref, direct_ref, pre_ref, taps_ref, out_ref
):
    rows, width, n = b0_ref.shape
    windows = ((p0_ref, b0_ref, m0_ref), (p1_ref, b1_ref, m1_ref))
    moves = [shifter(width, sc_ref[l]) for l in range(2)]

    def one(i, carry):
        at = pl.ds(pl.multiple_of(i * width, width), width)
        total = direct_ref[at, :]
        for l in range(2):
            for a in range(3):
                row = windows[l][a][i]
                moved = mm(moves[l], row)
                total = total + moved[width:] * taps_ref[l, 3 * a : 3 * a + 1, :]
                total = total + row.astype(F32) * taps_ref[l, 3 * a + 1 : 3 * a + 2, :]
                total = total + moved[:width] * taps_ref[l, 3 * a + 2 : 3 * a + 3, :]
        out_ref[i] = (total * slope(pre_ref[at, :])).astype(BF)
        return carry

    lax.fori_loop(0, rows, one, 0)


def gate(rates, b0, p0, m0, b1, p1, m1, direct, pre, depth):
    return pl.pallas_call(
        gate_kernel,
        in_specs=[SM] + [VM] * 9,
        out_specs=VM,
        out_shape=jax.ShapeDtypeStruct(b0.shape, BF),
        name="gate",
    )(rates, b0, p0, m0, b1, p1, m1, direct, pre, depth)


def grads_kernel(sc_ref, ext_ref, mid_ref, m_ref, later_ref, out_ref, g0, g1, g2, back):
    rate_row, rate_col = sc_ref[0], sc_ref[1]
    rows = ext_ref.shape[0] // 3
    width, n = ext_ref.shape[1:]
    c = mid_ref.shape[1]
    move = shifter(width, rate_col)

    def one(i, carry):
        at = pl.ds(pl.multiple_of(i * width, width), width)
        for a in range(3):
            row = ext_ref[rows + i - (a - 1) * rate_row]
            moved = mm(move, row).astype(BF)
            g0[at, a * n : (a + 1) * n] = moved[width:]
            g1[at, a * n : (a + 1) * n] = row
            g2[at, a * n : (a + 1) * n] = moved[:width]
        return carry

    lax.fori_loop(0, rows, one, 0)
    total = mm(g0[...], m_ref[0], NT) + mm(g1[...], m_ref[1], NT) + mm(g2[...], m_ref[2], NT)
    back[...] = total.astype(BF)
    out_ref[...] = jnp.zeros(out_ref.shape, F32)
    for k in range(3):
        lo, hi = k * n, min((k + 1) * n, c)
        out_ref[k, :c, : hi - lo] = mm(mid_ref[...], back[:, lo:hi], TN)
    for l in range(2):
        out_ref[3, l * n : (l + 1) * n, :] = later_ref[l]


def grads(rates, ext, mid, folded, later_grads):
    cells, c = mid.shape
    n = ext.shape[2]
    return pl.pallas_call(
        grads_kernel,
        in_specs=[SM] + [VM] * 4,
        out_specs=VM,
        out_shape=jax.ShapeDtypeStruct((4, 3 * n, n), F32),
        scratch_shapes=[pltpu.VMEM((cells, 3 * n), BF)] * 3 + [pltpu.VMEM((cells, c), BF)],
        name="grads",
    )(rates, ext, mid, folded, later_grads)


def row_windows(cells, rate):
    rows = cells.shape[0]

    def at(r):
        whole, rest = divmod(r, rows)

        def fetch(v):
            plus, minus = [], []
            plus.append(from_slab(v[rest:], whole) if whole else v[rest:])
            minus.append(from_slab(v[: rows - rest], -whole) if whole else v[: rows - rest])
            if rest:
                plus.append(from_slab(v[:rest], whole + 1))
                minus.insert(0, from_slab(v[rows - rest :], -whole - 1))
            return jnp.concatenate(plus), jnp.concatenate(minus)

        return fetch

    return lax.switch(rate - 1, [at(r) for r in range(1, 22)], cells)


def total_over_devices(parts):
    core = lax.axis_index("core")
    swap = [(0, 1), (1, 0)]
    blocks, rows, lanes = parts.shape
    half = blocks // 2
    chips = lax.axis_size(CHIPS)
    keep = lax.dynamic_slice_in_dim(parts, core * half, half, 0)
    give = lax.dynamic_slice_in_dim(parts, (1 - core) * half, half, 0).astype(BF)
    mine = (keep + lax.ppermute(give, "core", swap).astype(F32)).astype(BF)
    mine = mine.reshape(chips, half * rows // chips, lanes)
    pieces = lax.all_to_all(mine, CHIPS, split_axis=0, concat_axis=0, tiled=True)
    piece = jnp.sum(pieces.astype(F32), axis=0).astype(BF)
    whole = lax.all_to_all(
        jnp.broadcast_to(piece[None], mine.shape), CHIPS, split_axis=0, concat_axis=0, tiled=True
    ).reshape(half, rows, lanes)
    other = lax.ppermute(whole, "core", swap)
    first = jnp.where(core == 0, whole, other)
    second = jnp.where(core == 0, other, whole)
    return jnp.concatenate([first, second])


def local(
    features, upstream, depth_mid, point_mid, projection, depth_first, point_first,
    depth_later, point_later, joining, rate_first, rates_later,
):
    part = lax.axis_index("xh")
    _, rows, width, c = features.shape
    n = point_later.shape[1]
    cells = rows * width
    groups = lax.axis_size("z")
    down = from_slab(features[part, 0], 1)
    up = from_slab(features[part, rows - 1], -1)
    folded = fold_weights(projection, point_first, depth_first)
    tile = upstream[part].reshape(groups, rows, width // groups, n)
    slab = lax.all_to_all(tile, "z", split_axis=0, concat_axis=0, tiled=True)
    slab = slab.transpose(1, 0, 2, 3).reshape(cells, n)

    scalars = jnp.stack([part.astype(jnp.int32), rate_first[1]])
    mid, u0, us = front(scalars, features, up, down, depth_mid, point_mid, folded)
    us = us.reshape(2, rows, width, n)
    from_up = from_slab(us[0], -1)
    from_down = from_slab(us[1], 1)
    above = jnp.concatenate([from_up, us[0]])
    below = jnp.concatenate([us[1], from_down])
    above = lax.dynamic_slice_in_dim(above, rows - rate_first[0], rows, 0)
    below = lax.dynamic_slice_in_dim(below, rate_first[0], rows, 0)
    first_pre = u0.reshape(rows, width, n) + above.astype(F32) + below.astype(F32)
    first_out = jax.nn.silu(first_pre).astype(BF)

    p0, m0 = row_windows(first_out, rates_later[0, 0])
    p1, m1 = row_windows(first_out, rates_later[1, 0])
    cols = rates_later[:, 1]
    b0, b1, later_grads, direct = later(
        cols, first_out, p0, m0, p1, m1, slab, joining, depth_later, point_later
    )
    p0, m0 = row_windows(b0, rates_later[0, 0])
    p1, m1 = row_windows(b1, rates_later[1, 0])
    gated = gate(
        cols, b0, p0, m0, b1, p1, m1, direct, first_pre.reshape(cells, n), depth_later
    )
    ext = jnp.concatenate([from_slab(gated, -1), gated, from_slab(gated, 1)])
    parts = grads(rate_first, ext, mid, folded, later_grads)
    total = total_over_devices(parts).astype(F32)
    grad_mid = jnp.concatenate([total[0], total[1], total[2]], axis=1)[:c, :c]
    return grad_mid, total[3, : 2 * n].reshape(2, n, n)


def solution(mesh):
    section, rows, cols = mesh.devices.shape
    fine = Mesh(
        mesh.devices.reshape(section, rows // 4, 2, 2, cols), ("xh", "y", "xl", "core", "z")
    ) if hasattr(mesh, "devices") else mesh
    placed = (
        P(None, SLABS, None, None),
        P(None, ("y", "xl", "core"), "z", None),
    ) + (P(),) * 10
    return jax.shard_map(local, mesh=fine, in_specs=placed, out_specs=(P(), P()), check_vma=False)
```

```python
import jax
import jax.numpy as jnp
from jax import lax
from jax.experimental import pallas as pl
from jax.experimental.pallas import tpu as pltpu
from jax.sharding import Mesh, PartitionSpec as P

BF = jnp.bfloat16
F32 = jnp.float32
SLABS = ("y", "xl", "core", "z")
CHIPS = ("xh", "y", "xl", "z")
VM = pl.BlockSpec(memory_space=pltpu.VMEM)
SM = pl.BlockSpec(memory_space=pltpu.SMEM)
NN = (((1,), (0,)), ((), ()))
NT = (((1,), (1,)), ((), ()))
TN = (((0,), (0,)), ((), ()))


def mm(a, b, dims=NN):
    return lax.dot_general(a, b, dims, preferred_element_type=F32)


def sigmoid(v):
    return 1.0 / (1.0 + jnp.exp(-v))


def slope(v):
    s = sigmoid(v)
    return s * (1.0 + v * (1.0 - s))


def shifter(width, rate):
    j = lax.broadcasted_iota(jnp.int32, (2 * width, width), 0)
    c = lax.broadcasted_iota(jnp.int32, (2 * width, width), 1)
    want = jnp.where(j < width, j - rate, j - width + rate)
    return jnp.where(c == want, 1.0, 0.0).astype(BF)


def from_slab(value, shift, ring=False):
    count = lax.axis_size(SLABS)
    pairs = [(i, i - shift) for i in range(count) if 0 <= i - shift < count]
    if ring:
        pairs = [(i, (i - shift) % count) for i in range(count)]
    return lax.ppermute(value, SLABS, pairs)


def masked(window_ref, i, row, height):
    inside = jnp.logical_and(row + i >= 0, row + i < height)
    return window_ref[i] * jnp.where(inside, 1.0, 0.0).astype(BF)


def weights_kernel(proj_ref, point_ref, taps_ref, out_ref):
    n = point_ref.shape[1]
    taps = jnp.concatenate([taps_ref[...], jnp.zeros((7, taps_ref.shape[1]), F32)], axis=0).T
    for t in range(9):
        a, b = divmod(t, 3)
        scaled = (point_ref[...].astype(F32) * taps[:, t : t + 1]).astype(BF)
        out_ref[b, :, a * n : (a + 1) * n] = mm(proj_ref[...], scaled).astype(BF)


def fold_weights(projection, point_first, depth_first):
    c, ch = projection.shape
    b = point_first.shape[1]
    return pl.pallas_call(
        weights_kernel,
        in_specs=[VM] * 3,
        out_specs=VM,
        out_shape=jax.ShapeDtypeStruct((3, c, 3 * b), BF),
        cost_estimate=pl.CostEstimate(
            flops=18 * c * ch * b, bytes_accessed=8 * c * ch, transcendentals=0
        ),
        name="fold_weights",
    )(projection, point_first, depth_first)


def front_kernel(
    rate_ref, feat_ref, up_ref, dn_ref, taps_ref, point_ref, m_ref,
    mid_ref, u0_ref, above_ref, below_ref, act, so, left, right,
):
    part, rate = lax.axis_index("xh"), rate_ref[1]
    rows, width, c = feat_ref.shape[1:]
    zero = jnp.zeros((rows + 2, 8, c), F32)
    act[:, 0:8, :] = zero
    act[:, width + 8 : width + 16, :] = zero

    def activate(v):
        v = v.astype(F32)
        return v * sigmoid(v)

    act[0, 8 : width + 8, :] = activate(up_ref[...])
    act[rows + 1, 8 : width + 8, :] = activate(dn_ref[...])

    def fill(i, carry):
        act[i + 1, 8 : width + 8, :] = activate(feat_ref[part, i])
        return carry

    lax.fori_loop(0, rows, fill, 0)

    def conv(i, carry):
        at = pl.multiple_of(i * width, width)
        for lo in range(0, c, 128):
            hi = min(lo + 128, c)
            total = jnp.zeros((width, hi - lo), F32)
            for a in range(3):
                for b in range(3):
                    total = total + (
                        act[i + a, 7 + b : 7 + b + width, lo:hi]
                        * taps_ref[3 * a + b : 3 * a + b + 1, lo:hi]
                    )
            mid_ref[pl.ds(at, width), lo:hi] = total.astype(BF)
        return carry

    lax.fori_loop(0, rows, conv, 0)
    mixed = mm(mid_ref[...], point_ref[...])
    so[...] = (feat_ref[part].reshape(rows * width, c).astype(F32) + mixed).astype(BF)
    move = shifter(width, rate)

    def shift(i, carry):
        at = pl.ds(pl.multiple_of(i * width, width), width)
        moved = mm(move, so[at, :]).astype(BF)
        left[at, :] = moved[:width]
        right[at, :] = moved[width:]
        return carry

    lax.fori_loop(0, rows, shift, 0)
    n = u0_ref.shape[1]
    total = mm(left[...], m_ref[0]) + mm(so[...], m_ref[1]) + mm(right[...], m_ref[2])
    above_ref[...] = total[:, :n].astype(BF).reshape(rows, width, n)
    u0_ref[...] = total[:, n : 2 * n]
    below_ref[...] = total[:, 2 * n :].astype(BF).reshape(rows, width, n)


def front(rates, features, up, dn, depth_mid, point_mid, folded):
    _, rows, width, c = features.shape
    n = folded.shape[2] // 3
    cells = rows * width
    return pl.pallas_call(
        front_kernel,
        in_specs=[SM] + [VM] * 6,
        out_specs=[VM] * 4,
        out_shape=[
            jax.ShapeDtypeStruct((cells, c), BF),
            jax.ShapeDtypeStruct((cells, n), F32),
            jax.ShapeDtypeStruct((rows, width, n), BF),
            jax.ShapeDtypeStruct((rows, width, n), BF),
        ],
        scratch_shapes=[
            pltpu.VMEM((rows + 2, width + 16, c), F32),
            pltpu.VMEM((cells, c), BF),
            pltpu.VMEM((cells, c), BF),
            pltpu.VMEM((cells, c), BF),
        ],
        name="front",
    )(rates, features, up, dn, depth_mid, point_mid, folded)


def first_kernel(
    rate_ref, u0_ref, above_ref, below_ref, up_ref, dn_ref, pre_ref, out_ref, top_ref, end_ref
):
    rate = rate_ref[0]
    rows, width, n = out_ref.shape
    edge = rows // 2

    def one(i, carry):
        at = pl.ds(pl.multiple_of(i * width, width), width)
        high, low = i - rate, i + rate
        inner = above_ref[jnp.maximum(high, 0)].astype(F32)
        outer = up_ref[jnp.minimum(high + rows, rows - 1)].astype(F32)
        total = u0_ref[at, :] + jnp.where(high >= 0, inner, outer)
        inner = below_ref[jnp.minimum(low, rows - 1)].astype(F32)
        outer = dn_ref[jnp.maximum(low - rows, 0)].astype(F32)
        total = total + jnp.where(low < rows, inner, outer)
        pre_ref[at, :] = total
        out_ref[i] = (total * sigmoid(total)).astype(BF)
        return carry

    lax.fori_loop(0, rows, one, 0)
    top_ref[...] = out_ref[:edge]
    end_ref[...] = out_ref[rows - edge :]


def first(rates, u0, above, below, up, dn):
    rows, width, n = above.shape
    edge = rows // 2
    return pl.pallas_call(
        first_kernel,
        in_specs=[SM] + [VM] * 5,
        out_specs=[VM] * 4,
        out_shape=[
            jax.ShapeDtypeStruct((rows * width, n), F32),
            jax.ShapeDtypeStruct((rows, width, n), BF),
            jax.ShapeDtypeStruct((edge, width, n), BF),
            jax.ShapeDtypeStruct((edge, width, n), BF),
        ],
        name="first",
    )(rates, u0, above, below, up, dn)


def cut_kernel(sc_ref, up_ref, own_ref, dn_ref, p0_ref, m0_ref, p1_ref, m1_ref):
    many, rows, width, n = own_ref.shape
    edge = rows // 2
    outs = ((p0_ref, m0_ref), (p1_ref, m1_ref))

    def one(i, carry):
        for l in range(2):
            k = l % many
            rate = sc_ref[l, 0]
            rest = rate - (rate + edge - 1) // rows * rows
            for sign in (1, -1):
                j = i + sign * rest
                near = own_ref[k, jnp.clip(j, 0, rows - 1)]
                far = dn_ref[k, jnp.clip(j - rows, 0, edge - 1)]
                back = up_ref[k, jnp.clip(j + edge, 0, edge - 1)]
                row = jnp.where(j < 0, back, jnp.where(j < rows, near, far))
                outs[l][(1 - sign) // 2][i] = row
        return carry

    lax.fori_loop(0, rows, one, 0)


def cut(rates, up, own, dn):
    _, rows, width, n = own.shape
    return pl.pallas_call(
        cut_kernel,
        in_specs=[SM] + [VM] * 3,
        out_specs=[VM] * 4,
        out_shape=[jax.ShapeDtypeStruct((rows, width, n), BF)] * 4,
        name="cut",
    )(rates, up, own, dn)


def later_kernel(
    sc_ref, own_ref, p0_ref, m0_ref, p1_ref, m1_ref, up_ref, join_ref, taps_ref, point_ref,
    back_ref, top_ref, end_ref, grad_ref, direct_ref, conv,
):
    rows, width, n = own_ref.shape
    first, height = lax.axis_index(SLABS) * rows, lax.axis_size(SLABS) * rows
    windows = ((m0_ref, own_ref, p0_ref), (m1_ref, own_ref, p1_ref))
    for l in range(2):
        move = shifter(width, sc_ref[l, 1])

        def one(i, carry, l=l, move=move):
            total = jnp.zeros((width, n), F32)
            for a in range(3):
                row = masked(windows[l][a], i, first + (a - 1) * sc_ref[l, 0], height)
                moved = mm(move, row)
                total = total + moved[:width] * taps_ref[l, 3 * a : 3 * a + 1, :]
                total = total + row.astype(F32) * taps_ref[l, 3 * a + 1 : 3 * a + 2, :]
                total = total + moved[width:] * taps_ref[l, 3 * a + 2 : 3 * a + 3, :]
            conv[pl.ds(pl.multiple_of(i * width, width), width), :] = total.astype(BF)
            return carry

        lax.fori_loop(0, rows, one, 0)
        pre = mm(conv[...], point_ref[l])
        block = mm(up_ref[...], join_ref[(l + 1) * n : (l + 2) * n, :], NT)
        gate = (block * slope(pre)).astype(BF)
        back = mm(gate, point_ref[l], NT).astype(BF)
        back = back.reshape(rows, width, n)
        back_ref[l] = back
        top_ref[l] = back[: rows // 2]
        end_ref[l] = back[rows - rows // 2 :]
        grad_ref[l] = mm(conv[...], gate, TN)
    direct_ref[...] = mm(up_ref[...], join_ref[:n, :], NT)


def later(rates, own, windows, upstream, joining, depth, point):
    rows, width, n = own.shape
    cells = rows * width
    return pl.pallas_call(
        later_kernel,
        in_specs=[SM] + [VM] * 9,
        out_specs=[VM] * 5,
        out_shape=[
            jax.ShapeDtypeStruct((2, rows, width, n), BF),
            jax.ShapeDtypeStruct((2, rows // 2, width, n), BF),
            jax.ShapeDtypeStruct((2, rows // 2, width, n), BF),
            jax.ShapeDtypeStruct((2, n, n), F32),
            jax.ShapeDtypeStruct((cells, n), F32),
        ],
        scratch_shapes=[pltpu.VMEM((cells, n), BF)],
        name="later",
    )(rates, own, *windows, upstream, joining, depth, point)


def gate_kernel(
    sc_ref, own_ref, p0_ref, m0_ref, p1_ref, m1_ref, direct_ref, pre_ref, taps_ref, out_ref
):
    _, rows, width, n = own_ref.shape
    first, height = lax.axis_index(SLABS) * rows, lax.axis_size(SLABS) * rows
    windows = ((p0_ref, own_ref.at[0], m0_ref), (p1_ref, own_ref.at[1], m1_ref))
    moves = [shifter(width, sc_ref[l, 1]) for l in range(2)]

    def one(i, carry):
        at = pl.ds(pl.multiple_of(i * width, width), width)
        total = direct_ref[at, :]
        for l in range(2):
            for a in range(3):
                row = masked(windows[l][a], i, first - (a - 1) * sc_ref[l, 0], height)
                moved = mm(moves[l], row)
                total = total + moved[width:] * taps_ref[l, 3 * a : 3 * a + 1, :]
                total = total + row.astype(F32) * taps_ref[l, 3 * a + 1 : 3 * a + 2, :]
                total = total + moved[:width] * taps_ref[l, 3 * a + 2 : 3 * a + 3, :]
        out_ref[i] = (total * slope(pre_ref[at, :])).astype(BF)
        return carry

    lax.fori_loop(0, rows, one, 0)


def gate(rates, back, windows, direct, pre, depth):
    return pl.pallas_call(
        gate_kernel,
        in_specs=[SM] + [VM] * 8,
        out_specs=VM,
        out_shape=jax.ShapeDtypeStruct(back.shape[1:], BF),
        name="gate",
    )(rates, back, *windows, direct, pre, depth)


def grads_kernel(
    sc_ref, up_ref, own_ref, dn_ref, mid_ref, m_ref, later_ref, keep_ref, give_ref,
    g0, g1, g2, back,
):
    rate_row, rate_col = sc_ref[0], sc_ref[1]
    rows, width, n = own_ref.shape
    c = mid_ref.shape[1]
    move = shifter(width, rate_col)

    def one(i, carry):
        at = pl.ds(pl.multiple_of(i * width, width), width)
        for a in range(3):
            j = i - (a - 1) * rate_row
            row = own_ref[jnp.clip(j, 0, rows - 1)]
            if a == 0:
                row = jnp.where(j < rows, row, dn_ref[jnp.maximum(j - rows, 0)])
            if a == 2:
                row = jnp.where(j >= 0, row, up_ref[jnp.minimum(j + rows, rows - 1)])
            moved = mm(move, row).astype(BF)
            g0[at, a * n : (a + 1) * n] = moved[width:]
            g1[at, a * n : (a + 1) * n] = row
            g2[at, a * n : (a + 1) * n] = moved[:width]
        return carry

    lax.fori_loop(0, rows, one, 0)
    total = mm(g0[...], m_ref[0], NT) + mm(g1[...], m_ref[1], NT) + mm(g2[...], m_ref[2], NT)
    back[...] = total.astype(BF)
    core = lax.axis_index("core")

    def put(k, lo, hi, wide, value):
        @pl.when(core == k // 2)
        def _():
            keep_ref[k % 2, lo:hi, :wide] = value

        @pl.when(core != k // 2)
        def _():
            give_ref[k % 2, lo:hi, :wide] = value.astype(BF)

    keep_ref[:, c:, :] = jnp.zeros((2, keep_ref.shape[1] - c, n), F32)
    give_ref[:, c:, :] = jnp.zeros((2, keep_ref.shape[1] - c, n), BF)
    for k in range(3):
        lo, hi = k * n, min((k + 1) * n, c)
        part = mm(mid_ref[...], back[:, lo:hi], TN)
        if hi - lo < n:
            part = jnp.concatenate([part, jnp.zeros((c, n - hi + lo), F32)], axis=1)
        put(k, 0, c, n, part)
    for l in range(2):
        put(3, l * n, (l + 1) * n, n, later_ref[l])
    put(3, 2 * n, c, n, jnp.zeros((c - 2 * n, n), F32))


def grads(rates, up, own, dn, mid, folded, later_grads):
    cells, c = mid.shape
    n = own.shape[2]
    return pl.pallas_call(
        grads_kernel,
        in_specs=[SM] + [VM] * 6,
        out_specs=[VM] * 2,
        out_shape=[
            jax.ShapeDtypeStruct((2, 3 * n, n), F32),
            jax.ShapeDtypeStruct((2, 3 * n, n), BF),
        ],
        scratch_shapes=[pltpu.VMEM((cells, 3 * n), BF)] * 3 + [pltpu.VMEM((cells, c), BF)],
        name="grads",
    )(rates, up, own, dn, mid, folded, later_grads)


def row_windows(own, top, end, rates):
    rows = own.shape[1]
    below = from_slab(top, 1, ring=True)
    above = from_slab(end, -1, ring=True)
    p0, m0, p1, m1 = cut(rates, above, own, below)
    whole = (rates[:, 0] + rows // 2 - 1) // rows

    def at(q):
        def fetch(plus, minus):
            if q == 0:
                return plus, minus
            return from_slab(plus, q, ring=True), from_slab(minus, -q, ring=True)

        return fetch

    cases = [at(q) for q in range(4)]
    return lax.switch(whole[0], cases, p0, m0) + lax.switch(whole[1], cases, p1, m1)


def total_over_devices(keep, give):
    core = lax.axis_index("core")
    swap = [(0, 1), (1, 0)]
    half, rows, lanes = keep.shape
    chips = lax.axis_size(CHIPS)
    mine = (keep + lax.ppermute(give, "core", swap).astype(F32)).astype(BF)
    mine = mine.reshape(chips, half * rows // chips, lanes)

    def swapped(pieces):
        return lax.all_to_all(pieces, CHIPS, split_axis=0, concat_axis=0, tiled=True)

    piece = jnp.sum(swapped(mine).astype(F32), axis=0).astype(BF)
    whole = swapped(jnp.broadcast_to(piece[None], mine.shape)).reshape(half, rows, lanes)
    other = lax.ppermute(whole, "core", swap)
    first = jnp.where(core == 0, whole, other)
    second = jnp.where(core == 0, other, whole)
    return jnp.concatenate([first, second])


def local(
    features, upstream, depth_mid, point_mid, projection, depth_first, point_first,
    depth_later, point_later, joining, rate_first, rates_later,
):
    part = lax.axis_index("xh")
    _, rows, width, c = features.shape
    n = point_later.shape[1]
    cells = rows * width
    groups = lax.axis_size("z")
    down = from_slab(features[part, 0], 1)
    up = from_slab(features[part, rows - 1], -1)
    folded = fold_weights(projection, point_first, depth_first)
    tile = upstream[part].reshape(groups, rows, width // groups, n)
    slab = lax.all_to_all(tile, "z", split_axis=0, concat_axis=0, tiled=True)
    slab = slab.transpose(1, 0, 2, 3).reshape(cells, n)

    up, down, slab = lax.optimization_barrier((up, down, slab))
    mid, u0, above, below = front(
        rate_first, features, up, down, depth_mid, point_mid, folded
    )
    from_up = from_slab(above, -1)
    from_down = from_slab(below, 1)
    first_pre, first_out, top, end = first(rate_first, u0, above, below, from_up, from_down)
    windows = row_windows(first_out[None], top[None], end[None], rates_later)
    back, top, end, later_grads, direct = later(
        rates_later, first_out, windows, slab, joining, depth_later, point_later
    )
    windows = row_windows(back, top, end, rates_later)
    gated = gate(rates_later, back, windows, direct, first_pre, depth_later)
    keep, give = grads(
        rate_first, from_slab(gated, -1), gated, from_slab(gated, 1), mid, folded, later_grads
    )
    total = total_over_devices(keep, give).astype(F32)
    grad_mid = jnp.concatenate([total[0], total[1], total[2]], axis=1)[:c, :c]
    return grad_mid, total[3, : 2 * n].reshape(2, n, n)


def solution(mesh):
    section, rows, cols = mesh.devices.shape
    fine = Mesh(
        mesh.devices.reshape(section, rows // 4, 2, 2, cols), ("xh", "y", "xl", "core", "z")
    ) if hasattr(mesh, "devices") else mesh
    placed = (
        P(None, SLABS, None, None),
        P(None, ("y", "xl", "core"), "z", None),
    ) + (P(),) * 10
    return jax.shard_map(local, mesh=fine, in_specs=placed, out_specs=(P(), P()), check_vma=False)
```

```python
import jax
import jax.numpy as jnp
from jax import lax
from jax.experimental import pallas as pl
from jax.experimental.pallas import tpu as pltpu
from jax.sharding import Mesh, PartitionSpec as P

UNROLL = 6
BF = jnp.bfloat16
F32 = jnp.float32
SLABS = ("y", "xl", "core", "z")
CHIPS = ("xh", "y", "xl", "z")
VM = pl.BlockSpec(memory_space=pltpu.VMEM)
SM = pl.BlockSpec(memory_space=pltpu.SMEM)
NN = (((1,), (0,)), ((), ()))
NT = (((1,), (1,)), ((), ()))
TN = (((0,), (0,)), ((), ()))


def mm(a, b, dims=NN):
    return lax.dot_general(a, b, dims, preferred_element_type=F32)


def sigmoid(v):
    return 1.0 / (1.0 + jnp.exp(-v))


def slope(v):
    s = sigmoid(v)
    return s * (1.0 + v * (1.0 - s))


def shifter(width, rate):
    j = lax.broadcasted_iota(jnp.int32, (2 * width, width), 0)
    c = lax.broadcasted_iota(jnp.int32, (2 * width, width), 1)
    want = jnp.where(j < width, j - rate, j - width + rate)
    return jnp.where(c == want, 1.0, 0.0).astype(BF)


def from_slab(value, shift):
    count = lax.axis_size(SLABS)
    return lax.ppermute(value, SLABS, [(i, (i - shift) % count) for i in range(count)])


def swap_slabs(value, odd, ring=False):
    count = lax.axis_size(SLABS)
    pairs = [(i, i + 1 if i % 2 == odd else i - 1) for i in range(count)]
    if ring:
        pairs = [(i, j % count) for i, j in pairs]
    return lax.ppermute(value, SLABS, [(i, j) for i, j in pairs if 0 <= j < count])


def is_even():
    return lax.axis_index(SLABS) % 2 == 0


def inside(row, height):
    return jnp.where(jnp.logical_and(row >= 0, row < height), 1.0, 0.0)


def tap_sum(total, move, windows, i, row, step, height, taps, flip):
    width = total.shape[0]
    n = total.shape[1]
    lines = [windows[a][i] for a in range(3)]
    moved = mm(move, jnp.concatenate(lines, axis=1))
    low, high = (2, 0) if flip else (0, 2)
    for a in range(3):
        here = slice(a * n, (a + 1) * n)
        keep = inside(row + i + (a - 1) * step, height)
        w = [taps[3 * a + b : 3 * a + b + 1, :] * keep for b in range(3)]
        total = total + moved[:width, here] * w[low]
        total = total + lines[a].astype(F32) * w[1]
        total = total + moved[width:, here] * w[high]
    return total


def weights_kernel(proj_ref, point_ref, taps_ref, out_ref):
    n = point_ref.shape[1]
    taps = jnp.concatenate([taps_ref[...], jnp.zeros((7, taps_ref.shape[1]), F32)], axis=0).T
    for t in range(9):
        a, b = divmod(t, 3)
        scaled = (point_ref[...].astype(F32) * taps[:, t : t + 1]).astype(BF)
        out_ref[b, :, a * n : (a + 1) * n] = mm(proj_ref[...], scaled).astype(BF)


def fold_weights(projection, point_first, depth_first):
    c, ch = projection.shape
    b = point_first.shape[1]
    return pl.pallas_call(
        weights_kernel,
        in_specs=[VM] * 3,
        out_specs=VM,
        out_shape=jax.ShapeDtypeStruct((3, c, 3 * b), BF),
        cost_estimate=pl.CostEstimate(
            flops=18 * c * ch * b, bytes_accessed=8 * c * ch, transcendentals=0
        ),
        name="fold_weights",
    )(projection, point_first, depth_first)


def front_kernel(
    rate_ref, feat_ref, near_ref, other_ref, taps_ref, point_ref, m_ref,
    mid_ref, u0_ref, to_near_ref, to_other_ref, act, so, left, right,
):
    part, rate = lax.axis_index("xh"), rate_ref[1]
    rows, width, c = feat_ref.shape[1:]
    zero = jnp.zeros((rows + 2, 8, c), F32)
    act[:, 0:8, :] = zero
    act[:, width + 8 : width + 16, :] = zero

    def activate(v):
        v = v.astype(F32)
        return v * sigmoid(v)

    even = is_even()
    near, other = near_ref[...].astype(F32), other_ref[...].astype(F32)
    act[0, 8 : width + 8, :] = activate(jnp.where(even, other, near))
    act[rows + 1, 8 : width + 8, :] = activate(jnp.where(even, near, other))

    def fill(i, carry):
        act[i + 1, 8 : width + 8, :] = activate(feat_ref[part, i])
        return carry

    lax.fori_loop(0, rows, fill, 0)

    def conv(i, carry):
        at = pl.multiple_of(i * width, width)
        for lo in range(0, c, 128):
            hi = min(lo + 128, c)
            total = jnp.zeros((width, hi - lo), F32)
            for a in range(3):
                for b in range(3):
                    total = total + (
                        act[i + a, 7 + b : 7 + b + width, lo:hi]
                        * taps_ref[3 * a + b : 3 * a + b + 1, lo:hi]
                    )
            mid_ref[pl.ds(at, width), lo:hi] = total.astype(BF)
        return carry

    lax.fori_loop(0, rows, conv, 0)
    mixed = mm(mid_ref[...], point_ref[...])
    so[...] = (feat_ref[part].reshape(rows * width, c).astype(F32) + mixed).astype(BF)
    move = shifter(width, rate)

    def shift(i, carry):
        at = pl.ds(pl.multiple_of(i * width, width), width)
        moved = mm(move, so[at, :]).astype(BF)
        left[at, :] = moved[:width]
        right[at, :] = moved[width:]
        return carry

    lax.fori_loop(0, rows, shift, 0, unroll=3)
    n = u0_ref.shape[1]
    total = mm(left[...], m_ref[0]) + mm(so[...], m_ref[1]) + mm(right[...], m_ref[2])
    u0_ref[...] = total[:, n : 2 * n]
    above = total[:, :n].astype(BF).reshape(rows, width, n)
    below = total[:, 2 * n :].astype(BF).reshape(rows, width, n)

    @pl.when(even)
    def _():
        to_near_ref[...] = above
        to_other_ref[...] = below

    @pl.when(jnp.logical_not(even))
    def _():
        to_near_ref[...] = below
        to_other_ref[...] = above


def front(rates, features, up, dn, depth_mid, point_mid, folded):
    _, rows, width, c = features.shape
    n = folded.shape[2] // 3
    cells = rows * width
    return pl.pallas_call(
        front_kernel,
        in_specs=[SM] + [VM] * 6,
        out_specs=[VM] * 4,
        out_shape=[
            jax.ShapeDtypeStruct((cells, c), BF),
            jax.ShapeDtypeStruct((cells, n), F32),
            jax.ShapeDtypeStruct((rows, width, n), BF),
            jax.ShapeDtypeStruct((rows, width, n), BF),
        ],
        scratch_shapes=[
            pltpu.VMEM((rows + 2, width + 16, c), F32),
            pltpu.VMEM((cells, c), BF),
            pltpu.VMEM((cells, c), BF),
            pltpu.VMEM((cells, c), BF),
        ],
        name="front",
    )(rates, features, up, dn, depth_mid, point_mid, folded)


def first_kernel(
    rate_ref, u0_ref, near_ref, other_ref, of_near_ref, of_other_ref,
    pre_ref, out_ref, to_near_ref, to_other_ref,
):
    rate = rate_ref[0]
    rows, width, n = out_ref.shape
    edge = rows // 2
    even = is_even()

    def pick(even_ref, odd_ref, row):
        return jnp.where(even, even_ref[row], odd_ref[row])

    def one(i, carry):
        at = pl.ds(pl.multiple_of(i * width, width), width)
        high, low = i - rate, i + rate
        inner = pick(near_ref, other_ref, jnp.maximum(high, 0))
        outer = pick(of_other_ref, of_near_ref, jnp.minimum(high + rows, rows - 1))
        total = u0_ref[at, :] + jnp.where(high >= 0, inner, outer).astype(F32)
        inner = pick(other_ref, near_ref, jnp.minimum(low, rows - 1))
        outer = pick(of_near_ref, of_other_ref, jnp.maximum(low - rows, 0))
        total = total + jnp.where(low < rows, inner, outer).astype(F32)
        pre_ref[at, :] = total
        out_ref[i] = (total * sigmoid(total)).astype(BF)
        return carry

    lax.fori_loop(0, rows, one, 0)
    top, end = out_ref[:edge], out_ref[rows - edge :]
    to_near_ref[...] = jnp.where(even, end, top)
    to_other_ref[...] = jnp.where(even, top, end)


def first(rates, u0, near, other, of_near, of_other):
    rows, width, n = near.shape
    edge = rows // 2
    return pl.pallas_call(
        first_kernel,
        in_specs=[SM] + [VM] * 5,
        out_specs=[VM] * 4,
        out_shape=[
            jax.ShapeDtypeStruct((rows * width, n), F32),
            jax.ShapeDtypeStruct((rows, width, n), BF),
            jax.ShapeDtypeStruct((edge, width, n), BF),
            jax.ShapeDtypeStruct((edge, width, n), BF),
        ],
        name="first",
    )(rates, u0, near, other, of_near, of_other)


def cut_kernel(sc_ref, near_ref, own_ref, other_ref, p0_ref, m0_ref, p1_ref, m1_ref):
    many, rows, width, n = own_ref.shape
    edge = rows // 2
    outs = ((p0_ref, m0_ref), (p1_ref, m1_ref))
    even = is_even()

    def one(i, carry):
        for l in range(2):
            k = l % many
            rate = sc_ref[l, 0]
            rest = rate - (rate + edge - 1) // rows * rows
            for sign in (1, -1):
                j = i + sign * rest
                own = own_ref[k, jnp.clip(j, 0, rows - 1)]
                low = j < 0
                far = jnp.where(low, j + edge, jnp.clip(j - rows, 0, edge - 1))
                far = jnp.where(low == even, other_ref[k, far], near_ref[k, far])
                row = jnp.where(jnp.logical_and(j >= 0, j < rows), own, far)
                outs[l][(1 - sign) // 2][i] = row
        return carry

    lax.fori_loop(0, rows, one, 0)


def cut(rates, near, own, other):
    _, rows, width, n = own.shape
    return pl.pallas_call(
        cut_kernel,
        in_specs=[SM] + [VM] * 3,
        out_specs=[VM] * 4,
        out_shape=[jax.ShapeDtypeStruct((rows, width, n), BF)] * 4,
        name="cut",
    )(rates, near, own, other)


def later_kernel(
    sc_ref, own_ref, p0_ref, m0_ref, p1_ref, m1_ref, up_ref, join_ref, taps_ref, point_ref,
    back_ref, to_near_ref, to_other_ref, grad_ref, direct_ref, conv,
):
    rows, width, n = own_ref.shape
    first, height = lax.axis_index(SLABS) * rows, lax.axis_size(SLABS) * rows
    windows = ((m0_ref, own_ref, p0_ref), (m1_ref, own_ref, p1_ref))
    even = is_even()
    for l in range(2):
        move = shifter(width, sc_ref[l, 1])

        def one(i, carry, l=l, move=move):
            total = tap_sum(
                jnp.zeros((width, n), F32), move, windows[l], i, first, sc_ref[l, 0], height,
                taps_ref[l], False,
            )
            conv[pl.ds(pl.multiple_of(i * width, width), width), :] = total.astype(BF)
            return carry

        lax.fori_loop(0, rows, one, 0, unroll=UNROLL)
        pre = mm(conv[...], point_ref[l])
        block = mm(up_ref[...], join_ref[(l + 1) * n : (l + 2) * n, :], NT)
        gate = (block * slope(pre)).astype(BF)
        back = mm(gate, point_ref[l], NT).astype(BF)
        back = back.reshape(rows, width, n)
        back_ref[l] = back
        top, end = back[: rows // 2], back[rows - rows // 2 :]
        to_near_ref[l] = jnp.where(even, end, top)
        to_other_ref[l] = jnp.where(even, top, end)
        grad_ref[l] = mm(conv[...], gate, TN)
    direct_ref[...] = mm(up_ref[...], join_ref[:n, :], NT)


def later(rates, own, windows, upstream, joining, depth, point):
    rows, width, n = own.shape
    cells = rows * width
    return pl.pallas_call(
        later_kernel,
        in_specs=[SM] + [VM] * 9,
        out_specs=[VM] * 5,
        out_shape=[
            jax.ShapeDtypeStruct((2, rows, width, n), BF),
            jax.ShapeDtypeStruct((2, rows // 2, width, n), BF),
            jax.ShapeDtypeStruct((2, rows // 2, width, n), BF),
            jax.ShapeDtypeStruct((2, n, n), F32),
            jax.ShapeDtypeStruct((cells, n), F32),
        ],
        scratch_shapes=[pltpu.VMEM((cells, n), BF)],
        name="later",
    )(rates, own, *windows, upstream, joining, depth, point)


def gate_kernel(
    sc_ref, own_ref, p0_ref, m0_ref, p1_ref, m1_ref, direct_ref, pre_ref, taps_ref, out_ref
):
    _, rows, width, n = own_ref.shape
    first, height = lax.axis_index(SLABS) * rows, lax.axis_size(SLABS) * rows
    windows = ((p0_ref, own_ref.at[0], m0_ref), (p1_ref, own_ref.at[1], m1_ref))
    moves = [shifter(width, sc_ref[l, 1]) for l in range(2)]

    def one(i, carry):
        at = pl.ds(pl.multiple_of(i * width, width), width)
        total = direct_ref[at, :]
        for l in range(2):
            total = tap_sum(
                total, moves[l], windows[l], i, first, -sc_ref[l, 0], height, taps_ref[l], True
            )
        out_ref[i] = (total * slope(pre_ref[at, :])).astype(BF)
        return carry

    lax.fori_loop(0, rows, one, 0, unroll=2)


def gate(rates, back, windows, direct, pre, depth):
    return pl.pallas_call(
        gate_kernel,
        in_specs=[SM] + [VM] * 8,
        out_specs=VM,
        out_shape=jax.ShapeDtypeStruct(back.shape[1:], BF),
        name="gate",
    )(rates, back, *windows, direct, pre, depth)


def grads_kernel(
    sc_ref, near_ref, own_ref, other_ref, mid_ref, m_ref, later_ref, keep_ref, give_ref,
    g0, g1, g2, back,
):
    rate_row, rate_col = sc_ref[0], sc_ref[1]
    rows, width, n = own_ref.shape
    c = mid_ref.shape[1]
    even = is_even()
    move = shifter(width, rate_col)

    def one(i, carry):
        at = pl.ds(pl.multiple_of(i * width, width), width)
        for a in range(3):
            j = i - (a - 1) * rate_row
            row = own_ref[jnp.clip(j, 0, rows - 1)]
            if a == 0:
                far = jnp.maximum(j - rows, 0)
                row = jnp.where(j < rows, row, jnp.where(even, near_ref[far], other_ref[far]))
            if a == 2:
                far = jnp.minimum(j + rows, rows - 1)
                row = jnp.where(j >= 0, row, jnp.where(even, other_ref[far], near_ref[far]))
            moved = mm(move, row).astype(BF)
            g0[at, a * n : (a + 1) * n] = moved[width:]
            g1[at, a * n : (a + 1) * n] = row
            g2[at, a * n : (a + 1) * n] = moved[:width]
        return carry

    lax.fori_loop(0, rows, one, 0, unroll=UNROLL)
    total = mm(g0[...], m_ref[0], NT) + mm(g1[...], m_ref[1], NT) + mm(g2[...], m_ref[2], NT)
    back[...] = total.astype(BF)
    core = lax.axis_index("core")

    def put(k, lo, hi, wide, value):
        @pl.when(core == k // 2)
        def _():
            keep_ref[k % 2, lo:hi, :wide] = value.astype(BF)

        @pl.when(core != k // 2)
        def _():
            give_ref[k % 2, lo:hi, :wide] = value.astype(BF)

    keep_ref[:, c:, :] = jnp.zeros((2, keep_ref.shape[1] - c, n), BF)
    give_ref[:, c:, :] = jnp.zeros((2, keep_ref.shape[1] - c, n), BF)
    for k in range(3):
        lo, hi = k * n, min((k + 1) * n, c)
        part = mm(mid_ref[...], back[:, lo:hi], TN)
        if hi - lo < n:
            part = jnp.concatenate([part, jnp.zeros((c, n - hi + lo), F32)], axis=1)
        put(k, 0, c, n, part)
    for l in range(2):
        put(3, l * n, (l + 1) * n, n, later_ref[l])
    put(3, 2 * n, c, n, jnp.zeros((c - 2 * n, n), F32))


def grads(rates, up, own, dn, mid, folded, later_grads):
    cells, c = mid.shape
    n = own.shape[2]
    return pl.pallas_call(
        grads_kernel,
        in_specs=[SM] + [VM] * 6,
        out_specs=[VM] * 2,
        out_shape=[
            jax.ShapeDtypeStruct((2, 3 * n, n), BF),
            jax.ShapeDtypeStruct((2, 3 * n, n), BF),
        ],
        scratch_shapes=[pltpu.VMEM((cells, 3 * n), BF)] * 3 + [pltpu.VMEM((cells, c), BF)],
        name="grads",
    )(rates, up, own, dn, mid, folded, later_grads)


def row_windows(own, near, other, rates):
    rows = own.shape[1]
    near = swap_slabs(near, 0, ring=True)
    other = swap_slabs(other, 1, ring=True)
    p0, m0, p1, m1 = cut(rates, near, own, other)
    whole = (rates[:, 0] + rows // 2 - 1) // rows

    def at(q):
        def fetch(plus, minus):
            if q == 0:
                return plus, minus
            return from_slab(plus, q), from_slab(minus, -q)

        return fetch

    cases = [at(q) for q in range(4)]
    return lax.switch(whole[0], cases, p0, m0) + lax.switch(whole[1], cases, p1, m1)


def total_over_devices(keep, give):
    core = lax.axis_index("core")
    swap = [(0, 1), (1, 0)]
    half, rows, lanes = keep.shape
    chips = lax.axis_size(CHIPS)
    mine = (keep.astype(F32) + lax.ppermute(give, "core", swap).astype(F32)).astype(BF)
    mine = mine.reshape(chips, half * rows // chips, lanes)

    def swapped(pieces):
        return lax.all_to_all(pieces, CHIPS, split_axis=0, concat_axis=0, tiled=True)

    piece = jnp.sum(swapped(mine).astype(F32), axis=0).astype(BF)
    whole = swapped(jnp.broadcast_to(piece[None], mine.shape)).reshape(half, rows, lanes)
    other = lax.ppermute(whole, "core", swap)
    first = jnp.where(core == 0, whole, other)
    second = jnp.where(core == 0, other, whole)
    return jnp.concatenate([first, second])


def local(
    features, upstream, depth_mid, point_mid, projection, depth_first, point_first,
    depth_later, point_later, joining, rate_first, rates_later,
):
    part = lax.axis_index("xh")
    _, rows, width, c = features.shape
    n = point_later.shape[1]
    cells = rows * width
    groups = lax.axis_size("z")
    even = is_even()
    near = swap_slabs(features[part, jnp.where(even, rows - 1, 0)], 0)
    other = swap_slabs(features[part, jnp.where(even, 0, rows - 1)], 1)
    folded = fold_weights(projection, point_first, depth_first)
    tile = upstream[part].reshape(groups, rows, width // groups, n)
    slab = lax.all_to_all(tile, "z", split_axis=0, concat_axis=0, tiled=True)
    slab = slab.transpose(1, 0, 2, 3).reshape(cells, n)

    near, other, slab = lax.optimization_barrier((near, other, slab))
    mid, u0, near, other = front(
        rate_first, features, near, other, depth_mid, point_mid, folded
    )
    first_pre, first_out, near, other = first(
        rate_first, u0, near, other, swap_slabs(near, 0), swap_slabs(other, 1)
    )
    windows = row_windows(first_out[None], near[None], other[None], rates_later)
    back, near, other, later_grads, direct = later(
        rates_later, first_out, windows, slab, joining, depth_later, point_later
    )
    windows = row_windows(back, near, other, rates_later)
    gated = gate(rates_later, back, windows, direct, first_pre, depth_later)
    keep, give = grads(
        rate_first, swap_slabs(gated, 0), gated, swap_slabs(gated, 1), mid, folded, later_grads
    )
    total = total_over_devices(keep, give).astype(F32)
    grad_mid = jnp.concatenate([total[0], total[1], total[2]], axis=1)[:c, :c]
    return grad_mid, total[3, : 2 * n].reshape(2, n, n)


def solution(mesh):
    section, rows, cols = mesh.devices.shape
    fine = Mesh(
        mesh.devices.reshape(section, rows // 4, 2, 2, cols), ("xh", "y", "xl", "core", "z")
    ) if hasattr(mesh, "devices") else mesh
    placed = (
        P(None, SLABS, None, None),
        P(None, ("y", "xl", "core"), "z", None),
    ) + (P(),) * 10
    return jax.shard_map(local, mesh=fine, in_specs=placed, out_specs=(P(), P()), check_vma=False)
```

```python
import jax
import jax.numpy as jnp
from jax import lax
from jax.experimental import pallas as pl
from jax.experimental.pallas import tpu as pltpu
from jax.sharding import Mesh, PartitionSpec as P

UNROLL = 6
BF = jnp.bfloat16
F32 = jnp.float32
SLABS = ("y", "xl", "core", "z")
CHIPS = ("xh", "y", "xl", "z")
VM = pl.BlockSpec(memory_space=pltpu.VMEM)
SM = pl.BlockSpec(memory_space=pltpu.SMEM)
NN = (((1,), (0,)), ((), ()))
NT = (((1,), (1,)), ((), ()))
TN = (((0,), (0,)), ((), ()))


def mm(a, b, dims=NN):
    return lax.dot_general(a, b, dims, preferred_element_type=F32)


def sigmoid(v):
    return 1.0 / (1.0 + jnp.exp(-v))


def slope(v):
    s = sigmoid(v)
    return s * (1.0 + v * (1.0 - s))


def shifter(width, rate):
    j = lax.broadcasted_iota(jnp.int32, (2 * width, width), 0)
    c = lax.broadcasted_iota(jnp.int32, (2 * width, width), 1)
    want = jnp.where(j < width, j - rate, j - width + rate)
    return jnp.where(c == want, 1.0, 0.0).astype(BF)


def from_slab(value, shift):
    count = lax.axis_size(SLABS)
    return lax.ppermute(value, SLABS, [(i, (i - shift) % count) for i in range(count)])


def swap_slabs(value, odd, ring=False):
    count = lax.axis_size(SLABS)
    pairs = [(i, i + 1 if i % 2 == odd else i - 1) for i in range(count)]
    if ring:
        pairs = [(i, j % count) for i, j in pairs]
    return lax.ppermute(value, SLABS, [(i, j) for i, j in pairs if 0 <= j < count])


def is_even():
    return lax.axis_index(SLABS) % 2 == 0


def inside(row, height):
    return jnp.where(jnp.logical_and(row >= 0, row < height), 1.0, 0.0)


def tap_sum(total, move, windows, i, row, step, height, taps, flip):
    width = total.shape[0]
    n = total.shape[1]
    lines = [windows[a][i] for a in range(3)]
    moved = mm(move, jnp.concatenate(lines, axis=1))
    low, high = (2, 0) if flip else (0, 2)
    for a in range(3):
        here = slice(a * n, (a + 1) * n)
        keep = inside(row + i + (a - 1) * step, height)
        w = [taps[3 * a + b : 3 * a + b + 1, :] * keep for b in range(3)]
        total = total + moved[:width, here] * w[low]
        total = total + lines[a].astype(F32) * w[1]
        total = total + moved[width:, here] * w[high]
    return total


def weights_kernel(proj_ref, point_ref, taps_ref, out_ref):
    n = point_ref.shape[1]
    taps = jnp.concatenate([taps_ref[...], jnp.zeros((7, taps_ref.shape[1]), F32)], axis=0).T
    for t in range(9):
        a, b = divmod(t, 3)
        scaled = (point_ref[...].astype(F32) * taps[:, t : t + 1]).astype(BF)
        out_ref[b, :, a * n : (a + 1) * n] = mm(proj_ref[...], scaled).astype(BF)


def fold_weights(projection, point_first, depth_first):
    c, ch = projection.shape
    b = point_first.shape[1]
    return pl.pallas_call(
        weights_kernel,
        in_specs=[VM] * 3,
        out_specs=VM,
        out_shape=jax.ShapeDtypeStruct((3, c, 3 * b), BF),
        cost_estimate=pl.CostEstimate(
            flops=18 * c * ch * b, bytes_accessed=8 * c * ch, transcendentals=0
        ),
        name="fold_weights",
    )(projection, point_first, depth_first)


def front_kernel(
    rate_ref, feat_ref, near_ref, other_ref, taps_ref, point_ref, m_ref,
    mid_ref, u0_ref, to_near_ref, to_other_ref, act, so, left, right,
):
    part, rate = lax.axis_index("xh"), rate_ref[1]
    rows, width, c = feat_ref.shape[1:]
    zero = jnp.zeros((rows + 2, 8, c), F32)
    act[:, 0:8, :] = zero
    act[:, width + 8 : width + 16, :] = zero

    def activate(v):
        v = v.astype(F32)
        return v * sigmoid(v)

    even = is_even()
    near, other = near_ref[...].astype(F32), other_ref[...].astype(F32)
    act[0, 8 : width + 8, :] = activate(jnp.where(even, other, near))
    act[rows + 1, 8 : width + 8, :] = activate(jnp.where(even, near, other))

    def fill(i, carry):
        act[i + 1, 8 : width + 8, :] = activate(feat_ref[part, i])
        return carry

    lax.fori_loop(0, rows, fill, 0)

    def conv(i, carry):
        at = pl.multiple_of(i * width, width)
        for lo in range(0, c, 128):
            hi = min(lo + 128, c)
            total = jnp.zeros((width, hi - lo), F32)
            for a in range(3):
                for b in range(3):
                    total = total + (
                        act[i + a, 7 + b : 7 + b + width, lo:hi]
                        * taps_ref[3 * a + b : 3 * a + b + 1, lo:hi]
                    )
            mid_ref[pl.ds(at, width), lo:hi] = total.astype(BF)
        return carry

    lax.fori_loop(0, rows, conv, 0)
    mixed = mm(mid_ref[...], point_ref[...])
    so[...] = (feat_ref[part].reshape(rows * width, c).astype(F32) + mixed).astype(BF)
    move = shifter(width, rate)

    def shift(i, carry):
        at = pl.ds(pl.multiple_of(i * width, width), width)
        moved = mm(move, so[at, :]).astype(BF)
        left[at, :] = moved[:width]
        right[at, :] = moved[width:]
        return carry

    lax.fori_loop(0, rows, shift, 0, unroll=3)
    n = u0_ref.shape[1]
    total = mm(left[...], m_ref[0]) + mm(so[...], m_ref[1]) + mm(right[...], m_ref[2])
    u0_ref[...] = total[:, n : 2 * n]
    above = total[:, :n].astype(BF).reshape(rows, width, n)
    below = total[:, 2 * n :].astype(BF).reshape(rows, width, n)

    @pl.when(even)
    def _():
        to_near_ref[...] = above
        to_other_ref[...] = below

    @pl.when(jnp.logical_not(even))
    def _():
        to_near_ref[...] = below
        to_other_ref[...] = above


def front(rates, features, up, dn, depth_mid, point_mid, folded):
    _, rows, width, c = features.shape
    n = folded.shape[2] // 3
    cells = rows * width
    return pl.pallas_call(
        front_kernel,
        in_specs=[SM] + [VM] * 6,
        out_specs=[VM] * 4,
        out_shape=[
            jax.ShapeDtypeStruct((cells, c), BF),
            jax.ShapeDtypeStruct((cells, n), F32),
            jax.ShapeDtypeStruct((rows, width, n), BF),
            jax.ShapeDtypeStruct((rows, width, n), BF),
        ],
        scratch_shapes=[
            pltpu.VMEM((rows + 2, width + 16, c), F32),
            pltpu.VMEM((cells, c), BF),
            pltpu.VMEM((cells, c), BF),
            pltpu.VMEM((cells, c), BF),
        ],
        name="front",
    )(rates, features, up, dn, depth_mid, point_mid, folded)


def first_kernel(
    rate_ref, u0_ref, near_ref, other_ref, of_near_ref, of_other_ref,
    pre_ref, out_ref, to_near_ref, to_other_ref,
):
    rate = rate_ref[0]
    rows, width, n = out_ref.shape
    edge = rows // 2
    even = is_even()

    def pick(even_ref, odd_ref, row):
        return jnp.where(even, even_ref[row], odd_ref[row])

    def one(i, carry):
        at = pl.ds(pl.multiple_of(i * width, width), width)
        high, low = i - rate, i + rate
        inner = pick(near_ref, other_ref, jnp.maximum(high, 0))
        outer = pick(of_other_ref, of_near_ref, jnp.minimum(high + rows, rows - 1))
        total = u0_ref[at, :] + jnp.where(high >= 0, inner, outer).astype(F32)
        inner = pick(other_ref, near_ref, jnp.minimum(low, rows - 1))
        outer = pick(of_near_ref, of_other_ref, jnp.maximum(low - rows, 0))
        total = total + jnp.where(low < rows, inner, outer).astype(F32)
        pre_ref[at, :] = total
        out_ref[i] = (total * sigmoid(total)).astype(BF)
        return carry

    lax.fori_loop(0, rows, one, 0)
    top, end = out_ref[:edge], out_ref[rows - edge :]
    to_near_ref[...] = jnp.where(even, end, top)
    to_other_ref[...] = jnp.where(even, top, end)


def first(rates, u0, near, other, of_near, of_other):
    rows, width, n = near.shape
    edge = rows // 2
    return pl.pallas_call(
        first_kernel,
        in_specs=[SM] + [VM] * 5,
        out_specs=[VM] * 4,
        out_shape=[
            jax.ShapeDtypeStruct((rows * width, n), F32),
            jax.ShapeDtypeStruct((rows, width, n), BF),
            jax.ShapeDtypeStruct((edge, width, n), BF),
            jax.ShapeDtypeStruct((edge, width, n), BF),
        ],
        name="first",
    )(rates, u0, near, other, of_near, of_other)


def cut_kernel(sc_ref, near_ref, own_ref, other_ref, p0_ref, m0_ref, p1_ref, m1_ref):
    many, rows, width, n = own_ref.shape
    edge = rows // 2
    outs = ((p0_ref, m0_ref), (p1_ref, m1_ref))
    even = is_even()

    def one(i, carry):
        for l in range(2):
            k = l % many
            rate = sc_ref[l, 0]
            rest = rate - (rate + edge - 1) // rows * rows
            for sign in (1, -1):
                j = i + sign * rest
                own = own_ref[k, jnp.clip(j, 0, rows - 1)]
                low = j < 0
                far = jnp.where(low, j + edge, jnp.clip(j - rows, 0, edge - 1))
                far = jnp.where(low == even, other_ref[k, far], near_ref[k, far])
                row = jnp.where(jnp.logical_and(j >= 0, j < rows), own, far)
                outs[l][(1 - sign) // 2][i] = row
        return carry

    lax.fori_loop(0, rows, one, 0)


def cut(rates, near, own, other):
    _, rows, width, n = own.shape
    return pl.pallas_call(
        cut_kernel,
        in_specs=[SM] + [VM] * 3,
        out_specs=[VM] * 4,
        out_shape=[jax.ShapeDtypeStruct((rows, width, n), BF)] * 4,
        name="cut",
    )(rates, near, own, other)


def later_kernel(
    sc_ref, own_ref, p0_ref, m0_ref, p1_ref, m1_ref, up_ref, join_ref, taps_ref, point_ref,
    back_ref, to_near_ref, to_other_ref, grad_ref, direct_ref, conv,
):
    rows, width, n = own_ref.shape
    first, height = lax.axis_index(SLABS) * rows, lax.axis_size(SLABS) * rows
    windows = ((m0_ref, own_ref, p0_ref), (m1_ref, own_ref, p1_ref))
    even = is_even()
    for l in range(2):
        move = shifter(width, sc_ref[l, 1])

        def one(i, carry, l=l, move=move):
            total = tap_sum(
                jnp.zeros((width, n), F32), move, windows[l], i, first, sc_ref[l, 0], height,
                taps_ref[l], False,
            )
            conv[pl.ds(pl.multiple_of(i * width, width), width), :] = total.astype(BF)
            return carry

        lax.fori_loop(0, rows, one, 0, unroll=UNROLL)
        pre = mm(conv[...], point_ref[l])
        block = mm(up_ref[...], join_ref[(l + 1) * n : (l + 2) * n, :], NT)
        gate = (block * slope(pre)).astype(BF)
        back = mm(gate, point_ref[l], NT).astype(BF)
        back = back.reshape(rows, width, n)
        back_ref[l] = back
        top, end = back[: rows // 2], back[rows - rows // 2 :]
        to_near_ref[l] = jnp.where(even, end, top)
        to_other_ref[l] = jnp.where(even, top, end)
        grad_ref[l] = mm(conv[...], gate, TN)
    direct_ref[...] = mm(up_ref[...], join_ref[:n, :], NT)


def later(rates, own, windows, upstream, joining, depth, point):
    rows, width, n = own.shape
    cells = rows * width
    return pl.pallas_call(
        later_kernel,
        in_specs=[SM] + [VM] * 9,
        out_specs=[VM] * 5,
        out_shape=[
            jax.ShapeDtypeStruct((2, rows, width, n), BF),
            jax.ShapeDtypeStruct((2, rows // 2, width, n), BF),
            jax.ShapeDtypeStruct((2, rows // 2, width, n), BF),
            jax.ShapeDtypeStruct((2, n, n), F32),
            jax.ShapeDtypeStruct((cells, n), F32),
        ],
        scratch_shapes=[pltpu.VMEM((cells, n), BF)],
        name="later",
    )(rates, own, *windows, upstream, joining, depth, point)


def gate_kernel(
    sc_ref, own_ref, p0_ref, m0_ref, p1_ref, m1_ref, direct_ref, pre_ref, taps_ref, out_ref
):
    _, rows, width, n = own_ref.shape
    first, height = lax.axis_index(SLABS) * rows, lax.axis_size(SLABS) * rows
    windows = ((p0_ref, own_ref.at[0], m0_ref), (p1_ref, own_ref.at[1], m1_ref))
    moves = [shifter(width, sc_ref[l, 1]) for l in range(2)]

    def one(i, carry):
        at = pl.ds(pl.multiple_of(i * width, width), width)
        total = direct_ref[at, :]
        for l in range(2):
            total = tap_sum(
                total, moves[l], windows[l], i, first, -sc_ref[l, 0], height, taps_ref[l], True
            )
        out_ref[i] = (total * slope(pre_ref[at, :])).astype(BF)
        return carry

    lax.fori_loop(0, rows, one, 0, unroll=2)


def gate(rates, back, windows, direct, pre, depth):
    return pl.pallas_call(
        gate_kernel,
        in_specs=[SM] + [VM] * 8,
        out_specs=VM,
        out_shape=jax.ShapeDtypeStruct(back.shape[1:], BF),
        name="gate",
    )(rates, back, *windows, direct, pre, depth)


def grads_kernel(
    sc_ref, near_ref, own_ref, other_ref, mid_ref, m_ref, later_ref, keep_ref, give_ref,
    g0, g1, g2, back,
):
    rate_row, rate_col = sc_ref[0], sc_ref[1]
    rows, width, n = own_ref.shape
    c = mid_ref.shape[1]
    even = is_even()
    move = shifter(width, rate_col)

    def one(i, carry):
        at = pl.ds(pl.multiple_of(i * width, width), width)
        for a in range(3):
            j = i - (a - 1) * rate_row
            row = own_ref[jnp.clip(j, 0, rows - 1)]
            if a == 0:
                far = jnp.maximum(j - rows, 0)
                row = jnp.where(j < rows, row, jnp.where(even, near_ref[far], other_ref[far]))
            if a == 2:
                far = jnp.minimum(j + rows, rows - 1)
                row = jnp.where(j >= 0, row, jnp.where(even, other_ref[far], near_ref[far]))
            moved = mm(move, row).astype(BF)
            g0[at, a * n : (a + 1) * n] = moved[width:]
            g1[at, a * n : (a + 1) * n] = row
            g2[at, a * n : (a + 1) * n] = moved[:width]
        return carry

    lax.fori_loop(0, rows, one, 0, unroll=UNROLL)
    total = mm(g0[...], m_ref[0], NT) + mm(g1[...], m_ref[1], NT) + mm(g2[...], m_ref[2], NT)
    back[...] = total.astype(BF)
    core = lax.axis_index("core")

    def put(k, lo, hi, wide, value):
        @pl.when(core == k // 2)
        def _():
            keep_ref[k % 2, lo:hi, :wide] = value.astype(BF)

        @pl.when(core != k // 2)
        def _():
            give_ref[k % 2, lo:hi, :wide] = value.astype(BF)

    keep_ref[:, c:, :] = jnp.zeros((2, keep_ref.shape[1] - c, n), BF)
    give_ref[:, c:, :] = jnp.zeros((2, keep_ref.shape[1] - c, n), BF)
    for k in range(3):
        lo, hi = k * n, min((k + 1) * n, c)
        part = mm(mid_ref[...], back[:, lo:hi], TN)
        if hi - lo < n:
            part = jnp.concatenate([part, jnp.zeros((c, n - hi + lo), F32)], axis=1)
        put(k, 0, c, n, part)
    for l in range(2):
        put(3, l * n, (l + 1) * n, n, later_ref[l])
    put(3, 2 * n, c, n, jnp.zeros((c - 2 * n, n), F32))


def grads(rates, up, own, dn, mid, folded, later_grads):
    cells, c = mid.shape
    n = own.shape[2]
    return pl.pallas_call(
        grads_kernel,
        in_specs=[SM] + [VM] * 6,
        out_specs=[VM] * 2,
        out_shape=[
            jax.ShapeDtypeStruct((2, 3 * n, n), BF),
            jax.ShapeDtypeStruct((2, 3 * n, n), BF),
        ],
        scratch_shapes=[pltpu.VMEM((cells, 3 * n), BF)] * 3 + [pltpu.VMEM((cells, c), BF)],
        name="grads",
    )(rates, up, own, dn, mid, folded, later_grads)


def row_windows(own, near, other, rates):
    rows = own.shape[1]
    near = swap_slabs(near, 0, ring=True)
    other = swap_slabs(other, 1, ring=True)
    p0, m0, p1, m1 = cut(rates, near, own, other)
    whole = (rates[:, 0] + rows // 2 - 1) // rows

    def at(q):
        def fetch(plus, minus):
            if q == 0:
                return plus, minus
            return from_slab(plus, q), from_slab(minus, -q)

        return fetch

    cases = [at(q) for q in range(4)]
    return lax.switch(whole[0], cases, p0, m0) + lax.switch(whole[1], cases, p1, m1)


def total_over_devices(keep, give):
    core = lax.axis_index("core")
    swap = [(0, 1), (1, 0)]
    half, rows, lanes = keep.shape
    chips = lax.axis_size(CHIPS)
    mine = (keep.astype(F32) + lax.ppermute(give, "core", swap).astype(F32)).astype(BF)
    mine = mine.reshape(chips, half * rows // chips, lanes)

    def swapped(pieces):
        return lax.all_to_all(pieces, CHIPS, split_axis=0, concat_axis=0, tiled=True)

    piece = jnp.sum(swapped(mine).astype(F32), axis=0).astype(BF)
    whole = swapped(jnp.broadcast_to(piece[None], mine.shape)).reshape(half, rows, lanes)
    other = lax.ppermute(whole, "core", swap)
    low = core == 0
    return [jnp.where(low, whole[k], other[k]) for k in range(half)] + [
        jnp.where(low, other[k], whole[k]) for k in range(half)
    ]


def local(
    features, upstream, depth_mid, point_mid, projection, depth_first, point_first,
    depth_later, point_later, joining, rate_first, rates_later,
):
    part = lax.axis_index("xh")
    _, rows, width, c = features.shape
    n = point_later.shape[1]
    cells = rows * width
    groups = lax.axis_size("z")
    even = is_even()
    near = swap_slabs(features[part, jnp.where(even, rows - 1, 0)], 0)
    other = swap_slabs(features[part, jnp.where(even, 0, rows - 1)], 1)
    folded = fold_weights(projection, point_first, depth_first)
    mid, u0, near, other = front(
        rate_first, features, near, other, depth_mid, point_mid, folded
    )
    first_pre, first_out, near, other = first(
        rate_first, u0, near, other, swap_slabs(near, 0), swap_slabs(other, 1)
    )
    upstream, near, other = lax.optimization_barrier((upstream, near, other))
    tile = upstream[part].reshape(groups, rows, width // groups, n)
    slab = lax.all_to_all(tile, "z", split_axis=0, concat_axis=0, tiled=True)
    slab = slab.transpose(1, 0, 2, 3).reshape(cells, n)

    windows = row_windows(first_out[None], near[None], other[None], rates_later)
    back, near, other, later_grads, direct = later(
        rates_later, first_out, windows, slab, joining, depth_later, point_later
    )
    windows = row_windows(back, near, other, rates_later)
    gated = gate(rates_later, back, windows, direct, first_pre, depth_later)
    keep, give = grads(
        rate_first, swap_slabs(gated, 0), gated, swap_slabs(gated, 1), mid, folded, later_grads
    )
    *blocks, last = total_over_devices(keep, give)
    grad_mid = jnp.concatenate(blocks, axis=1)[:c, :c].astype(F32)
    return grad_mid, last[: 2 * n].reshape(2, n, n).astype(F32)


def solution(mesh):
    section, rows, cols = mesh.devices.shape
    fine = Mesh(
        mesh.devices.reshape(section, rows // 4, 2, 2, cols), ("xh", "y", "xl", "core", "z")
    ) if hasattr(mesh, "devices") else mesh
    placed = (
        P(None, SLABS, None, None),
        P(None, ("y", "xl", "core"), "z", None),
    ) + (P(),) * 10
    return jax.shard_map(local, mesh=fine, in_specs=placed, out_specs=(P(), P()), check_vma=False)
```
